32 devices in a mesh: groups: 2 (over y), shot: 8 (over z, x), slab: 2 (over core).
Axes of the slice: x: 2, y: 2, z: 4, core: 2. Of those that a mesh axis runs over, the one named last changes fastest.
Arguments:
- field_now: float32 [64, 8192], P('slab', ('groups', 'shot')), parts along dimension 1, may hold values from -6 to 6
- field_before: float32 [64, 8192], P('slab', ('groups', 'shot')), parts along dimension 1, may hold values from -6 to 6
- velocity: bfloat16 [64, 2048], P('slab', ('groups', 'shot')), parts along dimension 1, may hold values from 5 to 5.4375
- offsets: int32 [16], P(('groups', 'shot')), parts along dimension 0, may hold values from 0 to 512
- source_cell: int32 [16], P(('groups', 'shot')), parts along dimension 0, may hold values from 0 to 32767
- traces: bfloat16 [2, 4096, 256], P('slab', ('groups', 'shot')), parts along dimension 1, may hold values from -6 to 6
- trace_shot: int32 [2, 4096, 1], P('slab', ('groups', 'shot')), parts along dimension 1, may hold values from 0 to 7; in each aligned block of 256 rows (0 to 255, 256 to 511, ..., all dimensions but the last counted through in order) at most 64 rows name the same one
- trace_node_cell: int32 [2, 4096], P('slab', ('groups', 'shot')), parts along dimension 1, may hold values from 0 to 16383
Outputs:
- pressure: float32 [64, 8192], P('slab', ('groups', 'shot')), parts along dimension 1
The draws below stay inside these ranges and needn't reach their ends.
There are 2 independent parts, one for each index of `groups`. The reference program is written for one: setup_inputs(seed, part) draws one part's arguments, and reference() takes and returns one part's arrays. A program takes and returns all parts, laid end to end along the dimension named above; each array names one. Nothing has to cross between parts.
Inputs may be any that keep to these rules, and one draw needn't show every extreme that they name: `trace_shot`: among the trace rows of one device (aligned blocks of 256 rows along the second dimension, for each slab) at most 64 belong to one shot, and in some block some shot has exactly 64.
All inputs are finite; a program needn't handle non-finite values.
Results may differ from the reference program's by a relative error of at most 0.0003.
Values may be sent and summed in bfloat16 or wider, within the bound.
A program may use at most 64 MiB of HBM per device.

```python
import math
import jax
import jax.numpy as jnp
import numpy as np
from jax import lax

NS = 256
STEPS = 24
CZ = 32
W = 512
TR_DEV = 256
CAP = 64
NZ = 64
LX = 1024
N_SHOT = 8
N_SLAB = 2


def place_ends(array, stream_key, least, largest):
    longest = array.shape.index(max(array.shape))
    spots = []
    for shift in (0, 1):
        where = [jax.random.randint(jax.random.fold_in(stream_key, axis), (), 0, length) for axis, length in enumerate(array.shape)]
        where[longest] = (where[longest] + shift) % array.shape[longest]
        spots.append(tuple(where))
    return array.at[spots[0]].set(least).at[spots[1]].set(largest)


def shard_levels(rng, shape, shards, low, top_value):
    def one(axis_at, shards_of):
        heights = jax.random.uniform(jax.random.fold_in(jax.random.fold_in(rng, 6), axis_at), (shards_of,), jnp.float32, low / len(shards), top_value / len(shards))
        return jnp.repeat(jnp.exp(heights), shape[axis_at] // shards_of).reshape((-1,) + (1,) * (len(shape) - axis_at - 1))

    level = one(*shards[0])
    for cut in shards[1:]:
        level = level * one(*cut)
    return level


def shared_out(rng, own, number, rows, amount, top, bound, skew):
    sequence = jax.random.permutation(rng, amount)
    crowded, usual = shares(amount, rows * top, bound, skew, True), shares(amount, rows * top, bound, skew, False)
    places = jnp.arange(amount)

    def named(tallies, turn):
        used = int((tallies > 0).sum())
        fixed = max(1, used // 4)
        shifted = fixed + (places - fixed + turn * (used - fixed)) % max(1, amount - fixed)
        return jnp.zeros((amount,), jnp.int32).at[sequence[jnp.where(places < fixed, places, shifted)]].set(jnp.asarray(tallies, jnp.int32))

    tallies = jnp.where(number % 4 == 0, named(crowded, number // 4), named(usual, number - number // 4 - 1))
    mixed = jax.random.permutation(jax.random.fold_in(own, 3), amount)
    donor, receiver = mixed[0:amount // 2 * 2:2], mixed[1:amount // 2 * 2:2]
    room = jnp.minimum(tallies[donor] - 1, bound - tallies[receiver]) // 2
    room = jnp.where((donor == sequence[0]) | (receiver == sequence[0]) | (tallies[receiver] == 0), 0, jnp.maximum(room, 0))
    shifted = jax.random.randint(jax.random.fold_in(own, 4), (amount // 2,), 0, 1 << 20) % (room + 1)
    tallies = tallies.at[donor].add(-shifted).at[receiver].add(shifted)
    labels = jnp.searchsorted(jnp.cumsum(tallies), jnp.arange(rows * top), side="right").astype(jnp.int32)
    table = labels.reshape(top, rows).T
    table = table[jax.random.permutation(jax.random.fold_in(own, 1), rows)]
    turn = jax.random.randint(jax.random.fold_in(own, 2), (rows, 1), 0, top)
    return jnp.take_along_axis(table, (jnp.arange(top)[None, :] + turn) % top, axis=1)


def shares(amount, total, reach, skew, full):
    loads = [(1 << 20) // math.isqrt(rank ** skew) + 1 for rank in range(1, amount + 1)]
    largest = reach if full else min(reach, max(-(-total // amount), total * loads[0] // sum(loads)))
    least = 1 if total - largest >= amount - 1 else 0
    given, spare = [largest] + [least] * (amount - 1), total - largest - least * (amount - 1)
    while spare > 0:
        candidates = [i for i in range(1, amount) if given[i] < largest] or [i for i in range(1, amount) if given[i] < reach]
        whole, left = sum([loads[i] for i in candidates]), spare
        for i in candidates:
            addition = min(reach - given[i], max(1, left * loads[i] // whole), spare)
            given[i] = given[i] + addition
            spare = spare - addition
    return np.array(given)


def bell_draw(own_key, dims, deviation, limit, cuts=(), held_as=jnp.bfloat16):
    result = jax.random.normal(own_key, dims, jnp.float32) * deviation
    if len(cuts) > 0:
        result = shard_levels(own_key, dims, cuts, -0.22, 0.18) * result
    return jnp.clip(result, min=-limit, max=limit).astype(held_as)


def setup_inputs(seed: int = 0, part: int = 0) -> dict:
    keys = jax.random.split(jax.random.key(seed), 9)
    part_splits = jax.random.split(jax.random.fold_in(keys[8], part), 9)
    field_now = bell_draw(part_splits[0], (NZ, N_SHOT * W), 1.0, 6.0, ((0, 2), (1, 8)), jnp.float32)
    field_before = bell_draw(part_splits[1], (NZ, N_SHOT * W), 1.0, 6.0, ((0, 2), (1, 8)), jnp.float32)
    velocity = jnp.clip(5.0 + 0.4375 * jax.random.uniform(part_splits[2], (NZ, LX), jnp.float32) ** shard_levels(part_splits[2], (NZ, LX), ((0, 2), (1, 8)), -0.2, 0.2), 5.0, 5.4375).astype(jnp.bfloat16)
    offsets = place_ends(jax.random.randint(part_splits[3], (N_SHOT,), 0, LX - W + 1), jax.random.fold_in(part_splits[3], 1), 0, LX - W).astype(jnp.int32)
    source_cell = place_ends(jax.random.randint(part_splits[4], (N_SHOT,), 0, NZ * W), jax.random.fold_in(part_splits[4], 1), 0, (NZ * W) - 1).astype(jnp.int32)
    traces = bell_draw(part_splits[5], (N_SLAB, N_SHOT * TR_DEV, NS), 1.0, 6.0, ((0, 2), (1, 8)))
    trace_shot_keys = jax.random.split(jax.random.fold_in(part_splits[6], 1), N_SLAB * (N_SHOT * TR_DEV) // TR_DEV)
    trace_shot_turns = jax.random.permutation(jax.random.fold_in(part_splits[6], 3), N_SLAB * (N_SHOT * TR_DEV) // TR_DEV)
    trace_shot = jax.vmap(lambda own, number: shared_out(jax.random.fold_in(part_splits[6], 2), own, number, TR_DEV, N_SHOT, 1, CAP, 2))(trace_shot_keys, trace_shot_turns).reshape((N_SLAB, N_SHOT * TR_DEV, 1))
    trace_node_cell = place_ends(jax.random.randint(part_splits[7], (N_SLAB, N_SHOT * TR_DEV), 0, CZ * W), jax.random.fold_in(part_splits[7], 1), 0, (CZ * W) - 1).astype(jnp.int32)
    return dict(field_now=field_now, field_before=field_before, velocity=velocity, offsets=offsets, source_cell=source_cell, traces=traces, trace_shot=trace_shot, trace_node_cell=trace_node_cell)


LAP_CENTER = -205.0 / 72.0
LAP_TAPS = (1.6, -0.2, 8.0 / 315.0, -1.0 / 560.0)
PEAK = 0.12
DELAY = 5.0
SOURCE_GAIN = 2.0
RATIO = 0.1

def sample_table(sample_values, steps):
    kernel_step_index = jnp.arange(sample_values, dtype=jnp.float32)[:, None] + 0.5
    time_index = jnp.arange(steps, dtype=jnp.float32)[None, :] + 1.0
    return jnp.cos(math.pi * kernel_step_index * time_index / sample_values) * math.sqrt(2.0 / sample_values)

def ricker(step_value):
    argument = (math.pi * PEAK * (step_value - DELAY)) ** 2
    return (1.0 - 2.0 * argument) * jnp.exp(-argument)

def laplace(depth_padded, wavefield):
    depth_rows = wavefield.shape[-2]
    width_cols = wavefield.shape[-1]
    pads = [(0, 0)] * (wavefield.ndim - 1) + [(4, 4)]
    lateral_pad = jnp.pad(wavefield, pads)
    running_total = 2.0 * LAP_CENTER * wavefield
    for distance in range(1, 5):
        coeff = LAP_TAPS[distance - 1]
        running_total = running_total + coeff * (depth_padded[..., 4 + distance:4 + distance + depth_rows, :] + depth_padded[..., 4 - distance:4 - distance + depth_rows, :])
        running_total = running_total + coeff * (lateral_pad[..., 4 + distance:4 + distance + width_cols] + lateral_pad[..., 4 - distance:4 - distance + width_cols])
    return running_total

def reference(field_now, field_before, velocity, offsets, source_cell, traces, trace_shot, trace_node_cell):
    shots = offsets.shape[0]
    current = field_now.reshape(NZ, shots, W).transpose(1, 0, 2)
    previous = field_before.reshape(NZ, shots, W).transpose(1, 0, 2)
    column_index = offsets[:, None].astype(jnp.int32) + jnp.arange(W, dtype=jnp.int32)[None, :]
    window = jnp.take(velocity, column_index.reshape(-1), axis=1).reshape(NZ, shots, W).transpose(1, 0, 2)
    courant = jnp.square(window.astype(jnp.float32) * RATIO)
    table = sample_table(NS, STEPS)
    amplitude = jnp.dot(traces.reshape(-1, NS).astype(jnp.float32), table, precision=lax.Precision.HIGHEST)
    target = trace_shot.reshape(N_SLAB, -1).astype(jnp.int32)
    slabs = jnp.arange(N_SLAB, dtype=jnp.int32)[:, None]
    depth = slabs * CZ + trace_node_cell // W
    lateral = trace_node_cell % W
    flat_index = (target * (NZ * W) + depth * W + lateral).reshape(-1)
    cells = jnp.arange(NZ * W, dtype=jnp.int32)[None, :]
    source_mask = (cells == source_cell[:, None]).astype(jnp.float32).reshape(shots, NZ, W)

    def advance(step, carry):
        present, earlier = carry
        column = lax.dynamic_slice_in_dim(amplitude, step, 1, 1)[:, 0]
        injection = jnp.zeros((shots * NZ * W,), jnp.float32).at[flat_index].add(column).reshape(shots, NZ, W)
        injection = injection + SOURCE_GAIN * ricker(step.astype(jnp.float32)) * source_mask
        depth_padded = jnp.pad(present, ((0, 0), (4, 4), (0, 0)))
        advanced = 2.0 * present - earlier + courant * laplace(depth_padded, present) + injection
        return (advanced, present)
    current, previous = lax.fori_loop(0, STEPS, advance, (current, previous))
    return current.transpose(1, 0, 2).reshape(NZ, shots * W)
```

```python
import math

import jax
import jax.numpy as jnp
import numpy as np
from jax import lax
from jax.experimental import pallas as pl
from jax.experimental.pallas import tpu as pltpu
from jax.sharding import PartitionSpec as P

NS = 256
STEPS = 24
CAP = 64
LANES = 128
SUB = 8
ROWS = 32
CHUNK = 8

LAP_CENTER = -205.0 / 72.0
LAP_TAPS = (1.6, -0.2, 8.0 / 315.0, -1.0 / 560.0)
PEAK = 0.12
DELAY = 5.0
SOURCE_GAIN = 2.0
RATIO = 0.1
NT = (((1,), (1,)), ((), ()))
MESH = pl.DeviceIdType.MESH


def dot_nt(a, b):
    return lax.dot_general(a, b, NT, preferred_element_type=jnp.float32)


def dot_nn(a, b):
    return jnp.dot(a, b, preferred_element_type=jnp.float32)


def iota(shape, axis):
    return lax.broadcasted_iota(jnp.int32, shape, axis)


def ones_where(mask):
    return jnp.where(mask, 1.0, 0.0).astype(jnp.bfloat16)


def split3(x):
    high = x.astype(jnp.bfloat16)
    rest = x - high.astype(jnp.float32)
    middle = rest.astype(jnp.bfloat16)
    low = (rest - middle.astype(jnp.float32)).astype(jnp.bfloat16)
    return jnp.concatenate([high, middle, low], axis=0)


def sum3(parts):
    n = parts.shape[0] // 3
    return parts[0:n] + parts[n : 2 * n] + parts[2 * n : 3 * n]


def split_table():
    k = np.arange(NS, dtype=np.float64)[:, None] + 0.5
    t = np.arange(STEPS, dtype=np.float64)[None, :] + 1.0
    table = np.cos(math.pi * k * t / NS) * math.sqrt(2.0 / NS)
    rest = np.zeros((ROWS, NS), np.float32)
    rest[:STEPS] = table.T
    parts = []
    for _ in range(3):
        part = rest.astype(jnp.bfloat16)
        parts.append(part)
        rest = rest - part.astype(np.float32)
    return jnp.asarray(np.concatenate(parts, axis=0))


def ricker_value(step):
    a = (math.pi * PEAK * (step - DELAY)) ** 2
    return SOURCE_GAIN * (1.0 - 2.0 * a) * math.exp(-a)


def loop(start, stop, body, unrolled):
    if unrolled:
        for i in range(start, stop):
            body(i)
        return

    def one(i, carry):
        body(i)
        return carry

    lax.fori_loop(start, stop, one, 0)


def kernel(
    shots, slabs, table_hbm, now_hbm, before_hbm, velocity_hbm, traces_hbm, shot_hbm, node_hbm,
    offset_hbm, source_hbm, out_ref, offset_ref, source_ref,
    gathered, message, raw, panel_ref, table_ref, traces_ref, shot_ref, node_ref,
    perm, window, left, right, injection, first, second, scale, center,
    load_sem, send_sem, recv_sem, field_send, field_recv,
    relay_send, relay_recv,
):
    shot, slab = lax.axis_index("shot"), lax.axis_index("slab")
    depth, width = out_ref.shape
    rows = traces_ref.shape[0]
    columns = width // LANES
    groups = depth * slabs // SUB
    few = slabs <= 2 and shots <= 8

    def other_shot(d):
        return {"shot": lax.rem(shot + d, shots)}

    def other_slab(e):
        return {"slab": lax.rem(slab + e, slabs)}

    def load(i, source, to):
        return pltpu.make_async_copy(source, to, load_sem.at[i])

    load_traces = [
        load(0, traces_hbm, traces_ref), load(1, shot_hbm, shot_ref),
        load(2, node_hbm, node_ref), load(3, table_hbm, table_ref),
    ]
    load_panel = load(4, velocity_hbm, panel_ref)
    load_fields = [load(5, now_hbm, raw.at[slab, 0]), load(6, before_hbm, raw.at[slab, 1])]
    load_cells = [load(7, offset_hbm, offset_ref), load(8, source_hbm, source_ref)]
    for copy in load_traces + [load_panel] + load_fields + load_cells:
        copy.start()

    barrier = pltpu.get_barrier_semaphore()

    def greet_shot(d):
        pl.semaphore_signal(barrier, inc=1, device_id=other_shot(d), device_id_type=MESH)

    def greet_slab(e):
        pl.semaphore_signal(barrier, inc=1, device_id=other_slab(e), device_id_type=MESH)

    loop(1, slabs, greet_slab, few)
    loop(1, shots, greet_shot, few)

    def remote(source, to, send, recv, device):
        return pltpu.make_async_remote_copy(
            src_ref=source, dst_ref=to, send_sem=send, recv_sem=recv,
            device_id=device, device_id_type=MESH,
        )

    def field_copy(e, i):
        return remote(
            now_hbm if i == 0 else before_hbm, raw.at[slab, i],
            field_send.at[i, e], field_recv.at[i, e], other_slab(e),
        )

    def message_copy(d):
        return remote(
            message.at[lax.rem(shot + d, shots)], gathered.at[slab, shot],
            send_sem.at[d], recv_sem.at[d], other_shot(d),
        )

    def relay_copy(d, e):
        source = lax.rem(shot + shots - d, shots)
        return remote(
            gathered.at[slab, source], gathered.at[slab, source],
            relay_send.at[e, d], relay_recv.at[e, d], other_slab(e),
        )

    lane = iota((1, width), 1)
    spread_lane = (lane % LANES) * columns + lane // LANES
    perm[...] = ones_where(iota((width, width), 0) == spread_lane)
    ahead = ones_where(iota((rows, rows), 0) < iota((rows, rows), 1))
    for copy in load_cells:
        copy.wait()
    offset = offset_ref[0]
    first_cell = spread_lane + offset

    def open_window(s):
        begin = s * LANES
        if not isinstance(s, int):
            begin = pl.multiple_of(begin, LANES)
        window[pl.ds(begin, LANES), :] = ones_where(
            iota((LANES, width), 0) + begin == first_cell
        )

    loop(0, shots, open_window, few)

    pl.semaphore_wait(barrier, shots - 1 + slabs - 1)

    def start_fields(e):
        field_copy(e, 0).start()
        field_copy(e, 1).start()

    loop(1, slabs, start_fields, few)

    for copy in load_traces + [load_panel]:
        copy.wait()
    amplitude = sum3(dot_nt(table_ref[...], traces_ref[...]))
    node = node_ref[...]
    lateral = node % width
    row = iota((ROWS, rows), 0)
    where_to = jnp.where(
        row == STEPS, node // width,
        jnp.where(row == STEPS + 1, lateral // columns, lateral % columns),
    ).astype(jnp.float32)
    high = jnp.where(row < STEPS, amplitude, where_to).astype(jnp.bfloat16)
    low = jnp.where(row < STEPS, amplitude - high.astype(jnp.float32), where_to).astype(
        jnp.bfloat16
    )
    both = jnp.concatenate([high, low], axis=0)
    target = shot_ref[...]
    onehot = jnp.where(iota((shots, rows), 0) == target, 1.0, 0.0)
    count = dot_nn(onehot.astype(jnp.bfloat16), ahead)
    position = jnp.sum(onehot * count, axis=0, keepdims=True)
    slot = position + (target * CAP).astype(jnp.float32)
    at_slot = iota((LANES, rows), 0).astype(jnp.float32)
    low_half = iota((ROWS, LANES), 1) < CAP

    def fill(i):
        base = (i * LANES).astype(jnp.float32) if not isinstance(i, int) else float(i * LANES)
        picked = dot_nt(both, ones_where(at_slot == slot - base))
        highs, lows = picked[0:ROWS], picked[ROWS : 2 * ROWS]
        message[2 * i, 1] = panel_ref[...]
        message[2 * i + 1, 1] = panel_ref[...]
        message[2 * i, 0] = jnp.where(low_half, highs, pltpu.roll(lows, CAP, 1)).astype(jnp.bfloat16)
        message[2 * i + 1, 0] = jnp.where(low_half, pltpu.roll(highs, CAP, 1), lows).astype(
            jnp.bfloat16
        )

    loop(0, shots // 2, fill, few)
    loop(1, shots, lambda d: message_copy(d).start(), few)
    gathered[slab, shot] = message[shot]
    loop(1, slabs, lambda e: relay_copy(0, e).start(), few)

    def places(j):
        out = []
        for q in range(depth // SUB):
            at = j * depth + q * SUB
            out.append(pl.ds((at % groups) * SUB + at // groups, SUB, stride=SUB))
        return out

    def put(ref, j, values):
        for q, place in enumerate(places(j)):
            for c in range(columns):
                ref[c, place, :] = values[
                    q * SUB : (q + 1) * SUB, c * LANES : (c + 1) * LANES
                ]

    def put_fields(j):
        both_fields = jnp.concatenate([raw[j, 0], raw[j, 1]], axis=0)
        turned = sum3(dot_nn(split3(both_fields), perm[...]))
        put(first, j, turned[0:depth])
        put(second, j, turned[depth : 2 * depth])

    for copy in load_fields:
        copy.wait()
    put_fields(slab)

    row_depth = iota((depth, LANES), 0).astype(jnp.float32)
    at_lane = iota((LANES, LANES), 0).astype(jnp.float32)

    def build(e, d):
        half = e % 2
        j, s = lax.rem(slab + e, slabs), lax.rem(shot + shots - d, shots)
        lanes = pl.ds(d * LANES, LANES)
        if not isinstance(d, int):
            lanes = pl.ds(pl.multiple_of(d * LANES, LANES), LANES)
        values = gathered[j, s, 0].astype(jnp.float32)
        chosen = ones_where(row_depth == values[STEPS : STEPS + 1])
        for t in range(STEPS):
            spread = jnp.broadcast_to(values[t : t + 1], (depth, LANES)).astype(jnp.bfloat16)
            left[half, t * depth : (t + 1) * depth, lanes] = chosen * spread
        for c in range(columns):
            key = jnp.where(
                values[STEPS + 2 : STEPS + 3] == float(c), values[STEPS + 1 : STEPS + 2], -1.0
            )
            right[half, c * LANES : (c + 1) * LANES, lanes] = ones_where(at_lane == key)

    source = source_ref[0]
    source_depth, source_lateral = source // width, source % width
    source_column = (source_lateral % columns) * LANES + source_lateral // columns

    def put_injection(e, t0, steps):
        half = e % 2
        j = lax.rem(slab + e, slabs)
        product = dot_nt(left[half, t0 * depth : (t0 + steps) * depth, :], right[half])
        for q, place in enumerate(places(j)):
            at_source = jnp.where(
                (iota((SUB, width), 0) + (q * SUB + j * depth) == source_depth)
                & (iota((SUB, width), 1) == source_column),
                1.0, 0.0,
            )
            for t in range(steps):
                at = t * depth + q * SUB
                block = product[at : at + SUB] + ricker_value(float(t0 + t)) * at_source
                for c in range(columns):
                    injection[t0 + t, c, place, :] = block[:, c * LANES : (c + 1) * LANES]

    def arrive(d):
        message_copy(d).wait_recv()
        loop(1, slabs, lambda e: relay_copy(d, e).start(), few)
        build(0, d)

    build(0, 0)
    loop(1, shots, arrive, few)

    def wait_fields(e):
        field_copy(e, 0).wait()
        field_copy(e, 1).wait()
        put_fields(lax.rem(slab + slabs - e, slabs))

    loop(1, slabs, wait_fields, few)

    def put_courant(j):
        panel = jnp.concatenate(
            [gathered[j, s, 1] for s in range(shots)], axis=1
        )
        speed = dot_nn(panel, window[...]) * RATIO
        courant = speed * speed
        put(scale, j, courant * LAP_TAPS[0])
        put(center, j, courant * (2.0 * LAP_CENTER) + 2.0)

    put_courant(slab)
    put_injection(0, 0, STEPS)

    def advance(t, now, other):
        lane, sub = iota((SUB, LANES), 1), iota((SUB, LANES), 0)

        def cell(c, v):
            return now[c, v * SUB : (v + 1) * SUB, :]

        line = {(c, v): cell(c, v) for c in range(columns) for v in range(groups)}
        for c in range(columns):
            for k in range(4):
                line[c, groups + k] = jnp.where(
                    sub < SUB - 1, pltpu.roll(cell(c, k), SUB - 1, 0), 0.0
                )
                line[c, k - 4] = jnp.where(
                    sub > 0, pltpu.roll(cell(c, groups + k - 4), 1, 0), 0.0
                )
        for v in range(groups):
            mine = [line[c, v] for c in range(columns)]
            plus = [jnp.where(lane < LANES - 1, pltpu.roll(x, LANES - 1, 1), 0.0) for x in mine]
            minus = [jnp.where(lane > 0, pltpu.roll(x, 1, 1), 0.0) for x in mine]
            rows = slice(v * SUB, (v + 1) * SUB)
            for c in range(columns):
                total = None
                for k in range(1, 5):
                    after = mine[c + k] if c + k < columns else plus[c + k - columns]
                    prior = mine[c - k] if c >= k else minus[c - k + columns]
                    taps = (after + prior) + (line[c, v + k] + line[c, v - k])
                    if k == 1:
                        total = taps
                    else:
                        total = total + (LAP_TAPS[k - 1] / LAP_TAPS[0]) * taps
                other[c, rows, :] = (
                    (center[c, rows, :] * mine[c] - other[c, rows, :])
                    + scale[c, rows, :] * total
                    + injection[t, c, rows, :]
                )

    if few:
        for e in range(1, slabs):
            for d in range(shots):
                relay_copy(d, e).wait_recv()
                build(e, d)
            put_courant(lax.rem(slab + e, slabs))
            put_injection(e, 0, CHUNK)
        for t0 in range(0, STEPS, CHUNK):
            if t0 + CHUNK < STEPS:
                for e in range(1, slabs):
                    put_injection(e, t0 + CHUNK, CHUNK)
            for t in range(t0, t0 + CHUNK, 2):
                advance(t, first, second)
                advance(t + 1, second, first)
    else:
        def finish(e):
            loop(0, shots, lambda d: relay_copy(d, e).wait_recv(), False)

        def others(e):
            loop(0, shots, lambda d: build(e, d), False)
            put_courant(lax.rem(slab + e, slabs))
            put_injection(e, 0, STEPS)

        loop(1, slabs, finish, False)
        loop(1, slabs, others, False)

        def pair(i):
            advance(2 * i, first, second)
            advance(2 * i + 1, second, first)

        loop(0, STEPS // 2, pair, False)

    mine = jnp.concatenate(
        [
            jnp.concatenate([first[c, place, :] for c in range(columns)], axis=1)
            for place in places(slab)
        ],
        axis=0,
    )
    out_ref[...] = mine
    loop(1, shots, lambda d: message_copy(d).wait_send(), few)
    loop(0, shots, lambda d: loop(1, slabs, lambda e: relay_copy(d, e).wait_send(), few), few)


def restore(state_ref, out_ref):
    width = out_ref.shape[1]
    columns = width // LANES
    lane = iota((1, width), 1)
    spread_lane = (lane % LANES) * columns + lane // LANES
    perm = ones_where(iota((width, width), 0) == spread_lane)
    out_ref[...] = sum3(dot_nt(split3(state_ref[...]), perm))


def local(
    field_now, field_before, velocity, offsets, source_cell, traces, trace_shot, trace_node_cell
):
    depth, width = field_now.shape
    shots, slabs = lax.axis_size("shot"), lax.axis_size("slab")
    rows = traces.shape[1]
    columns = width // LANES
    cells = depth * slabs
    vmem = pl.BlockSpec(memory_space=pltpu.VMEM)
    hbm = pl.BlockSpec(memory_space=pltpu.HBM)
    dma = pltpu.SemaphoreType.DMA
    f32, bf16, i32 = jnp.float32, jnp.bfloat16, jnp.int32

    def body(*refs):
        kernel(shots, slabs, *refs)

    state = pl.pallas_call(
        body,
        out_shape=pltpu.VMEM((depth, width), f32),
        in_specs=[hbm] * 9,
        out_specs=vmem,
        scratch_shapes=[
            pltpu.SMEM((1,), i32),
            pltpu.SMEM((1,), i32),
            pltpu.VMEM((slabs, shots, 2, ROWS, LANES), bf16),
            pltpu.VMEM((shots, 2, ROWS, LANES), bf16),
            pltpu.VMEM((slabs, 2, depth, width), f32),
            pltpu.VMEM(velocity.shape, bf16),
            pltpu.VMEM((3 * ROWS, NS), bf16),
            pltpu.VMEM((rows, NS), bf16),
            pltpu.VMEM((1, rows), i32),
            pltpu.VMEM((1, rows), i32),
            pltpu.VMEM((width, width), bf16),
            pltpu.VMEM((shots * LANES, width), bf16),
            pltpu.VMEM((2, STEPS * depth, shots * LANES), bf16),
            pltpu.VMEM((2, width, shots * LANES), bf16),
            pltpu.VMEM((STEPS, columns, cells, LANES), f32),
            pltpu.VMEM((columns, cells, LANES), f32),
            pltpu.VMEM((columns, cells, LANES), f32),
            pltpu.VMEM((columns, cells, LANES), f32),
            pltpu.VMEM((columns, cells, LANES), f32),
            dma((9,)), dma((shots,)), dma((shots,)), dma((2, slabs)), dma((2, slabs)),
            dma((slabs, shots)), dma((slabs, shots)),
        ],
        compiler_params=pltpu.CompilerParams(
            collective_id=0, has_side_effects=True, vmem_limit_bytes=63 << 20
        ),
    )(
        split_table(), field_now, field_before, velocity, traces[0],
        trace_shot.reshape(1, rows), trace_node_cell, offsets, source_cell,
    )
    return pl.pallas_call(
        restore,
        out_shape=jax.ShapeDtypeStruct((depth, width), f32),
        in_specs=[vmem],
        out_specs=vmem,
        compiler_params=pltpu.CompilerParams(vmem_limit_bytes=16 << 20),
    )(state)


def solution(mesh):
    in_specs = (
        P("slab", ("groups", "shot")),
        P("slab", ("groups", "shot")),
        P("slab", ("groups", "shot")),
        P(("groups", "shot")),
        P(("groups", "shot")),
        P("slab", ("groups", "shot"), None),
        P("slab", ("groups", "shot"), None),
        P("slab", ("groups", "shot")),
    )
    out_specs = P("slab", ("groups", "shot"))
    return jax.shard_map(local, mesh=mesh, in_specs=in_specs, out_specs=out_specs, check_vma=False)
```

```python
import math

import jax
import jax.numpy as jnp
import numpy as np
from jax import lax
from jax.experimental import pallas as pl
from jax.experimental.pallas import tpu as pltpu
from jax.sharding import PartitionSpec as P

NS = 256
STEPS = 24
CAP = 64
LANES = 128
SUB = 8
ROWS = 32
CHUNK = 4
SCRATCH = 16

LAP_CENTER = -205.0 / 72.0
LAP_TAPS = (1.6, -0.2, 8.0 / 315.0, -1.0 / 560.0)
PEAK = 0.12
DELAY = 5.0
SOURCE_GAIN = 2.0
RATIO = 0.1
NT = (((1,), (1,)), ((), ()))
MESH = pl.DeviceIdType.MESH


def dot_nt(a, b):
    return lax.dot_general(a, b, NT, preferred_element_type=jnp.float32)


def dot_nn(a, b):
    return jnp.dot(a, b, preferred_element_type=jnp.float32)


def iota(shape, axis):
    return lax.broadcasted_iota(jnp.int32, shape, axis)


def ones_where(mask):
    return jnp.where(mask, 1.0, 0.0).astype(jnp.bfloat16)


def split3(x):
    high = x.astype(jnp.bfloat16)
    rest = x - high.astype(jnp.float32)
    middle = rest.astype(jnp.bfloat16)
    low = (rest - middle.astype(jnp.float32)).astype(jnp.bfloat16)
    return jnp.concatenate([high, middle, low], axis=0)


def sum3(parts):
    n = parts.shape[0] // 3
    return parts[0:n] + parts[n : 2 * n] + parts[2 * n : 3 * n]


def split_table():
    k = np.arange(NS, dtype=np.float64)[:, None] + 0.5
    t = np.arange(STEPS, dtype=np.float64)[None, :] + 1.0
    table = np.cos(math.pi * k * t / NS) * math.sqrt(2.0 / NS)
    rest = np.zeros((ROWS, NS), np.float32)
    rest[:STEPS] = table.T
    parts = []
    for _ in range(3):
        part = rest.astype(jnp.bfloat16)
        parts.append(part)
        rest = rest - part.astype(np.float32)
    return jnp.asarray(np.concatenate(parts, axis=0))


def ricker_value(step):
    a = (math.pi * PEAK * (step - DELAY)) ** 2
    return SOURCE_GAIN * (1.0 - 2.0 * a) * math.exp(-a)


def loop(start, stop, body, unrolled):
    if unrolled:
        for i in range(start, stop):
            body(i)
        return

    def one(i, carry):
        body(i)
        return carry

    lax.fori_loop(start, stop, one, 0)


def places(j, slabs, depth):
    groups = depth * slabs // SUB
    out = []
    for q in range(depth // SUB):
        at = j * depth + q * SUB
        out.append(pl.ds((at % groups) * SUB + at // groups, SUB, stride=SUB))
    return out


def source_at(source, columns):
    width = columns * LANES
    return source // width, source % width % columns, source % width // columns


def put_product(chunk, e, slabs, left, right, injection, extra):
    half, chunk_rows = e % 2, left.shape[1] // (STEPS // CHUNK)
    depth, columns = chunk_rows // (2 * CHUNK), right.shape[1] // LANES
    j = lax.rem(lax.axis_index("slab") + e, slabs)
    begin = chunk * chunk_rows
    product = dot_nt(left[half, begin : begin + chunk_rows, :], right[half])
    for q, place in enumerate(places(j, slabs, depth)):
        for t in range(CHUNK):
            at = 2 * t * depth + q * SUB
            block = product[at : at + SUB] + product[at + depth : at + depth + SUB]
            if extra is not None:
                block = block + ricker_value(float(chunk * CHUNK + t)) * extra[q]
            for c in range(columns):
                injection[t, c, place, :] = block[:, c * LANES : (c + 1) * LANES]


def exchange_kernel(
    shots, slabs, table_hbm, now_hbm, before_hbm, velocity_hbm, traces_hbm, shot_hbm, node_hbm,
    offset_ref, source_ref, *refs,
):
    few = slabs <= 2 and shots <= 8
    chunks = STEPS // CHUNK
    count = SCRATCH if few else SCRATCH + 2
    outs, scratch = refs[:-count], refs[-count:]
    first, second, scale, center, perm = outs[:5]
    injections = outs[5:6] if few else outs[5 : 5 + chunks]
    (
        left, right, gathered, message, raw, panel_ref, table_ref, traces_ref, shot_ref, node_ref,
        window, load_sem, send_sem, recv_sem, field_send, field_recv, relay_send, relay_recv,
    ) = (outs[6:8] + scratch) if few else scratch
    shot, slab = lax.axis_index("shot"), lax.axis_index("slab")
    depth, width = now_hbm.shape
    rows = traces_ref.shape[0]
    columns = width // LANES
    groups = depth * slabs // SUB

    def other_shot(d):
        return {"shot": lax.rem(shot + d, shots)}

    def other_slab(e):
        return {"slab": lax.rem(slab + e, slabs)}

    def load(i, source, to):
        return pltpu.make_async_copy(source, to, load_sem.at[i])

    load_traces = [
        load(0, traces_hbm, traces_ref), load(1, shot_hbm, shot_ref),
        load(2, node_hbm, node_ref), load(3, table_hbm, table_ref),
    ]
    load_panel = load(4, velocity_hbm, panel_ref)
    load_fields = [load(5, now_hbm, raw.at[slab, 0]), load(6, before_hbm, raw.at[slab, 1])]
    for copy in load_traces + [load_panel] + load_fields:
        copy.start()

    barrier = pltpu.get_barrier_semaphore()

    def greet_shot(d):
        pl.semaphore_signal(barrier, inc=1, device_id=other_shot(d), device_id_type=MESH)

    def greet_slab(e):
        pl.semaphore_signal(barrier, inc=1, device_id=other_slab(e), device_id_type=MESH)

    loop(1, slabs, greet_slab, few)
    loop(1, shots, greet_shot, few)

    def remote(source, to, send, recv, device):
        return pltpu.make_async_remote_copy(
            src_ref=source, dst_ref=to, send_sem=send, recv_sem=recv,
            device_id=device, device_id_type=MESH,
        )

    def field_copy(e, i):
        return remote(
            now_hbm if i == 0 else before_hbm, raw.at[slab, i],
            field_send.at[i, e], field_recv.at[i, e], other_slab(e),
        )

    def message_copy(d):
        return remote(
            message.at[lax.rem(shot + d, shots)], gathered.at[slab, shot],
            send_sem.at[d], recv_sem.at[d], other_shot(d),
        )

    def relay_copy(d, e):
        source = lax.rem(shot + shots - d, shots)
        return remote(
            gathered.at[slab, source], gathered.at[slab, source],
            relay_send.at[e, d], relay_recv.at[e, d], other_slab(e),
        )

    lane = iota((1, width), 1)
    spread_lane = (lane % LANES) * columns + lane // LANES
    perm[...] = ones_where(iota((width, width), 0) == spread_lane)
    ahead = ones_where(iota((rows, rows), 0) < iota((rows, rows), 1))
    offset = offset_ref[0]
    first_cell = spread_lane + offset

    def open_window(s):
        begin = s * LANES
        if not isinstance(s, int):
            begin = pl.multiple_of(begin, LANES)
        window[pl.ds(begin, LANES), :] = ones_where(
            iota((LANES, width), 0) + begin == first_cell
        )

    loop(0, shots, open_window, few)

    pl.semaphore_wait(barrier, shots - 1 + slabs - 1)

    def start_fields(e):
        field_copy(e, 0).start()
        field_copy(e, 1).start()

    loop(1, slabs, start_fields, few)

    for copy in load_traces + [load_panel]:
        copy.wait()
    amplitude = sum3(dot_nt(table_ref[...], traces_ref[...]))
    node = node_ref[...]
    lateral = node % width
    row = iota((ROWS, rows), 0)
    where_to = jnp.where(
        row == STEPS, node // width,
        jnp.where(row == STEPS + 1, lateral // columns, lateral % columns),
    ).astype(jnp.float32)
    high = jnp.where(row < STEPS, amplitude, where_to).astype(jnp.bfloat16)
    low = jnp.where(row < STEPS, amplitude - high.astype(jnp.float32), where_to).astype(
        jnp.bfloat16
    )
    both = jnp.concatenate([high, low], axis=0)
    target = shot_ref[...]
    onehot = jnp.where(iota((shots, rows), 0) == target, 1.0, 0.0)
    count = dot_nn(onehot.astype(jnp.bfloat16), ahead)
    position = jnp.sum(onehot * count, axis=0, keepdims=True)
    slot = position + (target * CAP).astype(jnp.float32)
    at_slot = iota((LANES, rows), 0).astype(jnp.float32)
    low_half = iota((ROWS, LANES), 1) < CAP

    def fill(i):
        base = (i * LANES).astype(jnp.float32) if not isinstance(i, int) else float(i * LANES)
        picked = dot_nt(both, ones_where(at_slot == slot - base))
        highs, lows = picked[0:ROWS], picked[ROWS : 2 * ROWS]
        message[2 * i, 1] = panel_ref[...]
        message[2 * i + 1, 1] = panel_ref[...]
        message[2 * i, 0] = jnp.where(low_half, highs, pltpu.roll(lows, CAP, 1)).astype(jnp.bfloat16)
        message[2 * i + 1, 0] = jnp.where(low_half, pltpu.roll(highs, CAP, 1), lows).astype(
            jnp.bfloat16
        )

    loop(0, shots // 2, fill, few)
    loop(1, shots, lambda d: message_copy(d).start(), few)
    gathered[slab, shot] = message[shot]
    loop(1, slabs, lambda e: relay_copy(0, e).start(), few)

    def put(ref, j, values):
        for q, place in enumerate(places(j, slabs, depth)):
            for c in range(columns):
                ref[c, place, :] = values[
                    q * SUB : (q + 1) * SUB, c * LANES : (c + 1) * LANES
                ]

    def put_fields(j):
        both_fields = jnp.concatenate([raw[j, 0], raw[j, 1]], axis=0)
        turned = sum3(dot_nn(split3(both_fields), perm[...]))
        put(first, j, turned[0:depth])
        put(second, j, turned[depth : 2 * depth])

    for copy in load_fields:
        copy.wait()
    put_fields(slab)

    row_depth = iota((depth, LANES), 0).astype(jnp.float32)
    at_lane = iota((LANES, LANES), 0).astype(jnp.float32)

    low_lanes = iota((ROWS, LANES), 1) < CAP

    def build(e, i):
        half = e % 2
        j = lax.rem(slab + e, slabs)
        lanes = pl.ds(i * LANES if isinstance(i, int) else pl.multiple_of(i * LANES, LANES), LANES)
        one = gathered[j, 2 * i, 0].astype(jnp.float32)
        two = gathered[j, 2 * i + 1, 0].astype(jnp.float32)
        parts = (
            jnp.where(low_lanes, one, pltpu.roll(two, CAP, 1)),
            jnp.where(low_lanes, pltpu.roll(one, CAP, 1), two),
        )
        chosen = ones_where(row_depth == parts[0][STEPS : STEPS + 1])
        for t in range(STEPS):
            for h in range(2):
                spread = jnp.broadcast_to(parts[h][t : t + 1], (depth, LANES))
                at = (2 * t + h) * depth
                left[half, at : at + depth, lanes] = chosen * spread.astype(jnp.bfloat16)
        lane_at, column_at = parts[0][STEPS + 1 : STEPS + 2], parts[0][STEPS + 2 : STEPS + 3]
        for c in range(columns):
            key = jnp.where(column_at == float(c), lane_at, -1.0)
            right[half, c * LANES : (c + 1) * LANES, lanes] = ones_where(at_lane == key)

    source_depth, source_column, source_lane = source_at(source_ref[0], columns)
    here = iota((SUB, width), 1) == source_column * LANES + source_lane

    def put_injection(e, chunk):
        j = lax.rem(slab + e, slabs)
        extra = [
            jnp.where((iota((SUB, width), 0) + (q * SUB + j * depth) == source_depth) & here, 1.0, 0.0)
            for q in range(depth // SUB)
        ]
        put_product(chunk, e, slabs, left, right, injections[chunk], extra)

    def arrive(s):
        d = lax.rem(shot + shots - s, shots)

        @pl.when(d > 0)
        def _():
            message_copy(d).wait_recv()
            loop(1, slabs, lambda e: relay_copy(d, e).start(), few)

    def arrive_pair(i):
        arrive(2 * i)
        arrive(2 * i + 1)
        build(0, i)

    loop(0, shots // 2, arrive_pair, few)

    def wait_fields(e):
        field_copy(e, 0).wait()
        field_copy(e, 1).wait()
        put_fields(lax.rem(slab + slabs - e, slabs))

    loop(1, slabs, wait_fields, few)

    def put_courant(j):
        panel = jnp.concatenate(
            [gathered[j, s, 1] for s in range(shots)], axis=1
        )
        speed = dot_nn(panel, window[...]) * RATIO
        courant = speed * speed
        put(scale, j, courant * LAP_TAPS[0])
        put(center, j, courant * (2.0 * LAP_CENTER) + 2.0)

    put_courant(slab)
    put_injection(0, 0)

    def relay_arrive(e, s):
        relay_copy(lax.rem(shot + shots - s, shots), e).wait_recv()

    def relay_pair(e, i):
        relay_arrive(e, 2 * i)
        relay_arrive(e, 2 * i + 1)
        build(e, i)

    if few:
        for e in range(1, slabs):
            loop(0, shots // 2, lambda i: relay_pair(e, i), True)
            put_courant(lax.rem(slab + e, slabs))
            put_injection(e, 0)
    else:
        for chunk in range(1, chunks):
            put_injection(0, chunk)

        def finish(e):
            loop(0, shots, lambda d: relay_copy(d, e).wait_recv(), False)

        def others(e):
            loop(0, shots // 2, lambda i: build(e, i), False)
            put_courant(lax.rem(slab + e, slabs))
            for chunk in range(chunks):
                put_injection(e, chunk)

        loop(1, slabs, finish, False)
        loop(1, slabs, others, False)
    loop(1, shots, lambda d: message_copy(d).wait_send(), few)
    loop(0, shots, lambda d: loop(1, slabs, lambda e: relay_copy(d, e).wait_send(), few), few)


def advance(injection, scale, center, t, now, earlier, later):
    columns, groups = now.shape[0], now.shape[1] // SUB
    lane, sub = iota((SUB, LANES), 1), iota((SUB, LANES), 0)

    def cell(c, v):
        return now[c, v * SUB : (v + 1) * SUB, :]

    line = {(c, v): cell(c, v) for c in range(columns) for v in range(groups)}
    for c in range(columns):
        for k in range(4):
            line[c, groups + k] = jnp.where(
                sub < SUB - 1, pltpu.roll(cell(c, k), SUB - 1, 0), 0.0
            )
            line[c, k - 4] = jnp.where(
                sub > 0, pltpu.roll(cell(c, groups + k - 4), 1, 0), 0.0
            )
    for v in range(groups):
        mine = [line[c, v] for c in range(columns)]
        plus = [jnp.where(lane < LANES - 1, pltpu.roll(x, LANES - 1, 1), 0.0) for x in mine]
        minus = [jnp.where(lane > 0, pltpu.roll(x, 1, 1), 0.0) for x in mine]
        rows = slice(v * SUB, (v + 1) * SUB)
        for c in range(columns):
            total = None
            for k in range(1, 5):
                after = mine[c + k] if c + k < columns else plus[c + k - columns]
                prior = mine[c - k] if c >= k else minus[c - k + columns]
                taps = (after + prior) + (line[c, v + k] + line[c, v - k])
                if k == 1:
                    total = taps
                else:
                    total = total + (LAP_TAPS[k - 1] / LAP_TAPS[0]) * taps
            later[c, rows, :] = (
                (center[c, rows, :] * mine[c] - earlier[c, rows, :])
                + scale[c, rows, :] * total
                + injection[t, c, rows, :]
            )


def wave_kernel(shots, slabs, source_ref, first, second, scale, center, perm, *refs):
    few = slabs <= 2 and shots <= 8
    chunks = STEPS // CHUNK
    if few:
        opening, left, right, out_ref = refs[:4]
        injections = (opening,) + refs[4 : 3 + chunks]
    else:
        injections, out_ref = refs[:chunks], refs[chunks]
    states = refs[-2:]
    depth, width = out_ref.shape
    columns = width // LANES
    groups = depth * slabs // SUB
    slab = lax.axis_index("slab")
    source_depth, source_column, source_lane = source_at(source_ref[0], columns)
    source_row = (source_depth % groups) * SUB + source_depth // groups
    here = iota((1, LANES), 1) == source_lane

    def prepare(chunk):
        injection = injections[chunk]
        for e in range(slabs):
            put_product(chunk, e, slabs, left, right, injection, None)
        for t in range(CHUNK):
            spot = pl.ds(source_row, 1)
            value = ricker_value(float(chunk * CHUNK + t))
            injection[t, source_column, spot, :] = injection[t, source_column, spot, :] + jnp.where(
                here, value, 0.0
            )

    for chunk in range(chunks):
        if few and chunk + 1 < chunks:
            prepare(chunk + 1)

        def step(t, now, before, after):
            advance(injections[chunk], scale, center, t, now, before, after)

        if chunk == 0:
            step(0, first, second, states[0])
            step(1, states[0], first, states[1])

        def pair(i):
            step(2 * i, states[1], states[0], states[0])
            step(2 * i + 1, states[0], states[1], states[1])

        loop(1 if chunk == 0 else 0, CHUNK // 2, pair, few)

    mine = jnp.concatenate(
        [
            jnp.concatenate([states[1][c, place, :] for c in range(columns)], axis=1)
            for place in places(slab, slabs, depth)
        ],
        axis=0,
    )
    out_ref[...] = sum3(dot_nt(split3(mine), perm[...]))


def local(
    field_now, field_before, velocity, offsets, source_cell, traces, trace_shot, trace_node_cell
):
    depth, width = field_now.shape
    shots, slabs = lax.axis_size("shot"), lax.axis_size("slab")
    rows = traces.shape[1]
    columns = width // LANES
    cells = depth * slabs
    vmem = pl.BlockSpec(memory_space=pltpu.VMEM)
    hbm = pl.BlockSpec(memory_space=pltpu.HBM)
    dma = pltpu.SemaphoreType.DMA
    f32, bf16, i32 = jnp.float32, jnp.bfloat16, jnp.int32

    chunks = STEPS // CHUNK
    few = slabs <= 2 and shots <= 8
    smem = pl.BlockSpec(memory_space=pltpu.SMEM)

    def exchange(*refs):
        exchange_kernel(shots, slabs, *refs)

    def wave(*refs):
        wave_kernel(shots, slabs, *refs)

    state = ((columns, cells, LANES), f32)
    injection = ((CHUNK, columns, cells, LANES), f32)
    factors = [
        ((2, STEPS * 2 * depth, shots * CAP), bf16),
        ((2, width, shots * CAP), bf16),
    ]
    passed = [state] * 4 + [((width, width), bf16)]
    passed += ([injection] + factors) if few else [injection] * chunks
    scratch = [] if few else [pltpu.VMEM(*factor) for factor in factors]
    scratch += [
        pltpu.VMEM((slabs, shots, 2, ROWS, LANES), bf16),
        pltpu.VMEM((shots, 2, ROWS, LANES), bf16),
        pltpu.VMEM((slabs, 2, depth, width), f32),
        pltpu.VMEM(velocity.shape, bf16),
        pltpu.VMEM((3 * ROWS, NS), bf16),
        pltpu.VMEM((rows, NS), bf16),
        pltpu.VMEM((1, rows), i32),
        pltpu.VMEM((1, rows), i32),
        pltpu.VMEM((shots * LANES, width), bf16),
        dma((7,)), dma((shots,)), dma((shots,)), dma((2, slabs)), dma((2, slabs)),
        dma((slabs, shots)), dma((slabs, shots)),
    ]
    held = sum(math.prod(shape) * jnp.dtype(kind).itemsize for shape, kind in passed)
    room = (63 << 20) - (held + (1 << 20) - 1 >> 20 << 20)
    prepared = pl.pallas_call(
        exchange,
        out_shape=[pltpu.VMEM(*each) for each in passed],
        in_specs=[hbm] * 7 + [smem] * 2,
        out_specs=[vmem] * len(passed),
        scratch_shapes=scratch,
        compiler_params=pltpu.CompilerParams(
            collective_id=0, has_side_effects=True, vmem_limit_bytes=room
        ),
    )(
        split_table(), field_now, field_before, velocity, traces[0],
        trace_shot.reshape(1, rows), trace_node_cell, offsets, source_cell,
    )
    later = [pltpu.VMEM(*injection)] * (chunks - 1) if few else []
    return pl.pallas_call(
        wave,
        out_shape=jax.ShapeDtypeStruct((depth, width), f32),
        in_specs=[smem] + [vmem] * len(passed),
        out_specs=vmem,
        scratch_shapes=later + [pltpu.VMEM(*state)] * 2,
        compiler_params=pltpu.CompilerParams(vmem_limit_bytes=32 << 20),
    )(source_cell, *prepared)


def solution(mesh):
    in_specs = (
        P("slab", ("groups", "shot")),
        P("slab", ("groups", "shot")),
        P("slab", ("groups", "shot")),
        P(("groups", "shot")),
        P(("groups", "shot")),
        P("slab", ("groups", "shot"), None),
        P("slab", ("groups", "shot"), None),
        P("slab", ("groups", "shot")),
    )
    out_specs = P("slab", ("groups", "shot"))
    return jax.shard_map(local, mesh=mesh, in_specs=in_specs, out_specs=out_specs, check_vma=False)
```

```python
import math

import jax
import jax.numpy as jnp
import numpy as np
from jax import lax
from jax.experimental import pallas as pl
from jax.experimental.pallas import tpu as pltpu
from jax.sharding import PartitionSpec as P

NS = 256
STEPS = 24
CAP = 64
LANES = 128
SUB = 8
ROWS = 32
CHUNK = 4
SCRATCH = 16

LAP_CENTER = -205.0 / 72.0
LAP_TAPS = (1.6, -0.2, 8.0 / 315.0, -1.0 / 560.0)
PEAK = 0.12
DELAY = 5.0
SOURCE_GAIN = 2.0
RATIO = 0.1
NT = (((1,), (1,)), ((), ()))
MESH = pl.DeviceIdType.MESH


def dot_nt(a, b):
    return lax.dot_general(a, b, NT, preferred_element_type=jnp.float32)


def dot_nn(a, b):
    return jnp.dot(a, b, preferred_element_type=jnp.float32)


def iota(shape, axis):
    return lax.broadcasted_iota(jnp.int32, shape, axis)


def ones_where(mask):
    return jnp.where(mask, 1.0, 0.0).astype(jnp.bfloat16)


def split3(x):
    high = x.astype(jnp.bfloat16)
    rest = x - high.astype(jnp.float32)
    middle = rest.astype(jnp.bfloat16)
    low = (rest - middle.astype(jnp.float32)).astype(jnp.bfloat16)
    return jnp.concatenate([high, middle, low], axis=0)


def sum3(parts):
    n = parts.shape[0] // 3
    return parts[0:n] + parts[n : 2 * n] + parts[2 * n : 3 * n]


def split_table():
    k = np.arange(NS, dtype=np.float64)[:, None] + 0.5
    t = np.arange(STEPS, dtype=np.float64)[None, :] + 1.0
    table = np.cos(math.pi * k * t / NS) * math.sqrt(2.0 / NS)
    rest = np.zeros((ROWS, NS), np.float32)
    rest[:STEPS] = table.T
    parts = []
    for _ in range(3):
        part = rest.astype(jnp.bfloat16)
        parts.append(part)
        rest = rest - part.astype(np.float32)
    return jnp.asarray(np.concatenate(parts, axis=0))


def ricker_value(step):
    a = (math.pi * PEAK * (step - DELAY)) ** 2
    return SOURCE_GAIN * (1.0 - 2.0 * a) * math.exp(-a)


def loop(start, stop, body, unrolled):
    if unrolled:
        for i in range(start, stop):
            body(i)
        return

    def one(i, carry):
        body(i)
        return carry

    lax.fori_loop(start, stop, one, 0)


def places(j, slabs, depth):
    groups = depth * slabs // SUB
    out = []
    for q in range(depth // SUB):
        at = j * depth + q * SUB
        out.append(pl.ds((at % groups) * SUB + at // groups, SUB, stride=SUB))
    return out


def source_at(source, columns):
    width = columns * LANES
    return source // width, source % width % columns, source % width // columns


def put_product(chunk, e, slabs, left, right, injection, extra):
    half, chunk_rows = e % 2, left.shape[1] // (STEPS // CHUNK)
    depth, columns = chunk_rows // (2 * CHUNK), right.shape[1] // LANES
    j = lax.rem(lax.axis_index("slab") + e, slabs)
    begin = chunk * chunk_rows
    product = dot_nt(left[half, begin : begin + chunk_rows, :], right[half])
    for q, place in enumerate(places(j, slabs, depth)):
        for t in range(CHUNK):
            at = 2 * t * depth + q * SUB
            block = product[at : at + SUB] + product[at + depth : at + depth + SUB]
            if extra is not None:
                block = block + ricker_value(float(chunk * CHUNK + t)) * extra[q]
            for c in range(columns):
                injection[t, c, place, :] = block[:, c * LANES : (c + 1) * LANES]


def exchange_kernel(
    shots, slabs, table_hbm, now_hbm, before_hbm, velocity_hbm, traces_hbm, shot_hbm, node_hbm,
    offset_ref, source_ref, *refs,
):
    few = slabs <= 2 and shots <= 8
    chunks = STEPS // CHUNK
    count = SCRATCH if few else SCRATCH + 2
    outs, scratch = refs[:-count], refs[-count:]
    first, second, scale, center, perm = outs[:5]
    injections = outs[5:6] if few else outs[5 : 5 + chunks]
    (
        left, right, gathered, message, raw, panel_ref, table_ref, traces_ref, shot_ref, node_ref,
        window, load_sem, send_sem, recv_sem, field_send, field_recv, relay_send, relay_recv,
    ) = (outs[6:8] + scratch) if few else scratch
    shot, slab = lax.axis_index("shot"), lax.axis_index("slab")
    depth, width = now_hbm.shape
    rows = traces_ref.shape[0]
    columns = width // LANES
    groups = depth * slabs // SUB

    def other_shot(d):
        return {"shot": lax.rem(shot + d, shots)}

    def other_slab(e):
        return {"slab": lax.rem(slab + e, slabs)}

    def load(i, source, to):
        return pltpu.make_async_copy(source, to, load_sem.at[i])

    load_traces = [
        load(0, traces_hbm, traces_ref), load(1, shot_hbm, shot_ref),
        load(2, node_hbm, node_ref), load(3, table_hbm, table_ref),
    ]
    load_panel = load(4, velocity_hbm, panel_ref)
    load_fields = [load(5, now_hbm, raw.at[slab, 0]), load(6, before_hbm, raw.at[slab, 1])]
    for copy in load_traces + [load_panel] + load_fields:
        copy.start()

    barrier = pltpu.get_barrier_semaphore()

    def greet_shot(d):
        pl.semaphore_signal(barrier, inc=1, device_id=other_shot(d), device_id_type=MESH)

    def greet_slab(e):
        pl.semaphore_signal(barrier, inc=1, device_id=other_slab(e), device_id_type=MESH)

    loop(1, slabs, greet_slab, few)
    loop(1, shots, greet_shot, few)

    def remote(source, to, send, recv, device):
        return pltpu.make_async_remote_copy(
            src_ref=source, dst_ref=to, send_sem=send, recv_sem=recv,
            device_id=device, device_id_type=MESH,
        )

    def field_copy(e, i):
        return remote(
            now_hbm if i == 0 else before_hbm, raw.at[slab, i],
            field_send.at[i, e], field_recv.at[i, e], other_slab(e),
        )

    def message_copy(d):
        return remote(
            message.at[lax.rem(shot + d, shots)], gathered.at[slab, shot],
            send_sem.at[d], recv_sem.at[d], other_shot(d),
        )

    def relay_copy(d, e):
        source = lax.rem(shot + shots - d, shots)
        return remote(
            gathered.at[slab, source], gathered.at[slab, source],
            relay_send.at[e, d], relay_recv.at[e, d], other_slab(e),
        )

    lane = iota((1, width), 1)
    spread_lane = (lane % LANES) * columns + lane // LANES
    perm[...] = ones_where(iota((width, width), 0) == spread_lane)
    ahead = ones_where(iota((rows, rows), 0) < iota((rows, rows), 1))
    offset = offset_ref[0]
    first_cell = spread_lane + offset

    def open_window(s):
        begin = s * LANES
        if not isinstance(s, int):
            begin = pl.multiple_of(begin, LANES)
        window[pl.ds(begin, LANES), :] = ones_where(
            iota((LANES, width), 0) + begin == first_cell
        )

    loop(0, shots, open_window, few)

    for copy in load_traces + [load_panel]:
        copy.wait()
    amplitude = sum3(dot_nt(table_ref[...], traces_ref[...]))
    node = node_ref[...]
    lateral = node % width
    row = iota((ROWS, rows), 0)
    where_to = jnp.where(
        row == STEPS, node // width,
        jnp.where(row == STEPS + 1, lateral // columns, lateral % columns),
    ).astype(jnp.float32)
    high = jnp.where(row < STEPS, amplitude, where_to).astype(jnp.bfloat16)
    low = jnp.where(row < STEPS, amplitude - high.astype(jnp.float32), where_to).astype(
        jnp.bfloat16
    )
    both = jnp.concatenate([high, low], axis=0)
    target = shot_ref[...]
    onehot = jnp.where(iota((shots, rows), 0) == target, 1.0, 0.0)
    count = dot_nn(onehot.astype(jnp.bfloat16), ahead)
    position = jnp.sum(onehot * count, axis=0, keepdims=True)
    slot = position + (target * CAP).astype(jnp.float32)
    at_slot = iota((LANES, rows), 0).astype(jnp.float32)
    low_half = iota((ROWS, LANES), 1) < CAP

    def fill(i):
        base = (i * LANES).astype(jnp.float32) if not isinstance(i, int) else float(i * LANES)
        picked = dot_nt(both, ones_where(at_slot == slot - base))
        highs, lows = picked[0:ROWS], picked[ROWS : 2 * ROWS]
        message[2 * i, 1] = panel_ref[...]
        message[2 * i + 1, 1] = panel_ref[...]
        message[2 * i, 0] = jnp.where(low_half, highs, pltpu.roll(lows, CAP, 1)).astype(jnp.bfloat16)
        message[2 * i + 1, 0] = jnp.where(low_half, pltpu.roll(highs, CAP, 1), lows).astype(
            jnp.bfloat16
        )

    loop(0, shots // 2, fill, few)
    pl.semaphore_wait(barrier, shots - 1 + slabs - 1)
    loop(1, shots, lambda d: message_copy(d).start(), few)

    def start_fields(e):
        field_copy(e, 0).start()
        field_copy(e, 1).start()

    loop(1, slabs, start_fields, few)
    gathered[slab, shot] = message[shot]
    loop(1, slabs, lambda e: relay_copy(0, e).start(), few)

    def put(ref, j, values):
        for q, place in enumerate(places(j, slabs, depth)):
            for c in range(columns):
                ref[c, place, :] = values[
                    q * SUB : (q + 1) * SUB, c * LANES : (c + 1) * LANES
                ]

    def put_fields(j):
        both_fields = jnp.concatenate([raw[j, 0], raw[j, 1]], axis=0)
        turned = sum3(dot_nn(split3(both_fields), perm[...]))
        put(first, j, turned[0:depth])
        put(second, j, turned[depth : 2 * depth])

    for copy in load_fields:
        copy.wait()
    put_fields(slab)

    row_depth = iota((depth, LANES), 0).astype(jnp.float32)
    at_lane = iota((LANES, LANES), 0).astype(jnp.float32)

    low_lanes = iota((ROWS, LANES), 1) < CAP

    def build(e, i):
        half = e % 2
        j = lax.rem(slab + e, slabs)
        lanes = pl.ds(i * LANES if isinstance(i, int) else pl.multiple_of(i * LANES, LANES), LANES)
        one = gathered[j, 2 * i, 0].astype(jnp.float32)
        two = gathered[j, 2 * i + 1, 0].astype(jnp.float32)
        parts = (
            jnp.where(low_lanes, one, pltpu.roll(two, CAP, 1)),
            jnp.where(low_lanes, pltpu.roll(one, CAP, 1), two),
        )
        chosen = ones_where(row_depth == parts[0][STEPS : STEPS + 1])
        for t in range(STEPS):
            for h in range(2):
                spread = jnp.broadcast_to(parts[h][t : t + 1], (2 * SUB, LANES))
                spread = spread.astype(jnp.bfloat16)
                for part in range(0, depth, 2 * SUB):
                    at = (2 * t + h) * depth + part
                    left[half, at : at + 2 * SUB, lanes] = (
                        chosen[part : part + 2 * SUB] * spread
                    )
        lane_at, column_at = parts[0][STEPS + 1 : STEPS + 2], parts[0][STEPS + 2 : STEPS + 3]
        for c in range(columns):
            key = jnp.where(column_at == float(c), lane_at, -1.0)
            right[half, c * LANES : (c + 1) * LANES, lanes] = ones_where(at_lane == key)

    source_depth, source_column, source_lane = source_at(source_ref[0], columns)
    here = iota((SUB, width), 1) == source_column * LANES + source_lane

    def put_injection(e, chunk):
        j = lax.rem(slab + e, slabs)
        extra = [
            jnp.where((iota((SUB, width), 0) + (q * SUB + j * depth) == source_depth) & here, 1.0, 0.0)
            for q in range(depth // SUB)
        ]
        put_product(chunk, e, slabs, left, right, injections[chunk], extra)

    def arrive(s):
        d = lax.rem(shot + shots - s, shots)

        @pl.when(d > 0)
        def _():
            message_copy(d).wait_recv()
            loop(1, slabs, lambda e: relay_copy(d, e).start(), few)

    def arrive_pair(i):
        arrive(2 * i)
        arrive(2 * i + 1)
        build(0, i)

    loop(0, shots // 2, arrive_pair, few)

    def wait_fields(e):
        field_copy(e, 0).wait()
        field_copy(e, 1).wait()
        put_fields(lax.rem(slab + slabs - e, slabs))

    loop(1, slabs, wait_fields, few)

    def put_courant(j):
        panel = jnp.concatenate(
            [gathered[j, s, 1] for s in range(shots)], axis=1
        )
        speed = dot_nn(panel, window[...]) * RATIO
        courant = speed * speed
        put(scale, j, courant * LAP_TAPS[0])
        put(center, j, courant * (2.0 * LAP_CENTER) + 2.0)

    put_courant(slab)
    put_injection(0, 0)

    def relay_arrive(e, s):
        relay_copy(lax.rem(shot + shots - s, shots), e).wait_recv()

    def relay_pair(e, i):
        relay_arrive(e, 2 * i)
        relay_arrive(e, 2 * i + 1)
        build(e, i)

    if few:
        for e in range(1, slabs):
            loop(0, shots // 2, lambda i: relay_pair(e, i), True)
            put_courant(lax.rem(slab + e, slabs))
            put_injection(e, 0)
    else:
        for chunk in range(1, chunks):
            put_injection(0, chunk)

        def finish(e):
            loop(0, shots, lambda d: relay_copy(d, e).wait_recv(), False)

        def others(e):
            loop(0, shots // 2, lambda i: build(e, i), False)
            put_courant(lax.rem(slab + e, slabs))
            for chunk in range(chunks):
                put_injection(e, chunk)

        loop(1, slabs, finish, False)
        loop(1, slabs, others, False)
    loop(1, shots, lambda d: message_copy(d).wait_send(), few)
    loop(0, shots, lambda d: loop(1, slabs, lambda e: relay_copy(d, e).wait_send(), few), few)


def advance(injection, scale, center, t, now, earlier, later):
    columns, groups = now.shape[0], now.shape[1] // SUB
    lane, sub = iota((SUB, LANES), 1), iota((SUB, LANES), 0)

    def cell(c, v):
        return now[c, v * SUB : (v + 1) * SUB, :]

    line = {(c, v): cell(c, v) for c in range(columns) for v in range(groups)}
    for c in range(columns):
        for k in range(4):
            line[c, groups + k] = jnp.where(
                sub < SUB - 1, pltpu.roll(cell(c, k), SUB - 1, 0), 0.0
            )
            line[c, k - 4] = jnp.where(
                sub > 0, pltpu.roll(cell(c, groups + k - 4), 1, 0), 0.0
            )
    for v in range(groups):
        mine = [line[c, v] for c in range(columns)]
        plus = [jnp.where(lane < LANES - 1, pltpu.roll(x, LANES - 1, 1), 0.0) for x in mine]
        minus = [jnp.where(lane > 0, pltpu.roll(x, 1, 1), 0.0) for x in mine]
        rows = slice(v * SUB, (v + 1) * SUB)
        for c in range(columns):
            total = None
            for k in range(1, 5):
                after = mine[c + k] if c + k < columns else plus[c + k - columns]
                prior = mine[c - k] if c >= k else minus[c - k + columns]
                taps = (after + prior) + (line[c, v + k] + line[c, v - k])
                if k == 1:
                    total = taps
                else:
                    total = total + (LAP_TAPS[k - 1] / LAP_TAPS[0]) * taps
            later[c, rows, :] = (
                (center[c, rows, :] * mine[c] - earlier[c, rows, :])
                + scale[c, rows, :] * total
                + injection[t, c, rows, :]
            )


def wave_kernel(shots, slabs, source_ref, first, second, scale, center, perm, *refs):
    few = slabs <= 2 and shots <= 8
    chunks = STEPS // CHUNK
    if few:
        opening, left, right, out_ref = refs[:4]
        injections = (opening,) + refs[4 : 3 + chunks]
    else:
        injections, out_ref = refs[:chunks], refs[chunks]
    states = refs[-2:]
    depth, width = out_ref.shape
    columns = width // LANES
    groups = depth * slabs // SUB
    slab = lax.axis_index("slab")
    source_depth, source_column, source_lane = source_at(source_ref[0], columns)
    source_row = (source_depth % groups) * SUB + source_depth // groups
    here = iota((1, LANES), 1) == source_lane

    def prepare(chunk):
        injection = injections[chunk]
        for e in range(slabs):
            put_product(chunk, e, slabs, left, right, injection, None)
        for t in range(CHUNK):
            spot = pl.ds(source_row, 1)
            value = ricker_value(float(chunk * CHUNK + t))
            injection[t, source_column, spot, :] = injection[t, source_column, spot, :] + jnp.where(
                here, value, 0.0
            )

    for chunk in range(chunks):
        if few and chunk + 1 < chunks:
            prepare(chunk + 1)

        def step(t, now, before, after):
            advance(injections[chunk], scale, center, t, now, before, after)

        if chunk == 0:
            step(0, first, second, states[0])
            step(1, states[0], first, states[1])

        def pair(i):
            step(2 * i, states[1], states[0], states[0])
            step(2 * i + 1, states[0], states[1], states[1])

        loop(1 if chunk == 0 else 0, CHUNK // 2, pair, few)

    mine = jnp.concatenate(
        [
            jnp.concatenate([states[1][c, place, :] for c in range(columns)], axis=1)
            for place in places(slab, slabs, depth)
        ],
        axis=0,
    )
    out_ref[...] = sum3(dot_nt(split3(mine), perm[...]))


def local(
    field_now, field_before, velocity, offsets, source_cell, traces, trace_shot, trace_node_cell
):
    depth, width = field_now.shape
    shots, slabs = lax.axis_size("shot"), lax.axis_size("slab")
    rows = traces.shape[1]
    columns = width // LANES
    cells = depth * slabs
    vmem = pl.BlockSpec(memory_space=pltpu.VMEM)
    hbm = pl.BlockSpec(memory_space=pltpu.HBM)
    dma = pltpu.SemaphoreType.DMA
    f32, bf16, i32 = jnp.float32, jnp.bfloat16, jnp.int32

    chunks = STEPS // CHUNK
    few = slabs <= 2 and shots <= 8
    smem = pl.BlockSpec(memory_space=pltpu.SMEM)

    def exchange(*refs):
        exchange_kernel(shots, slabs, *refs)

    def wave(*refs):
        wave_kernel(shots, slabs, *refs)

    state = ((columns, cells, LANES), f32)
    injection = ((CHUNK, columns, cells, LANES), f32)
    factors = [
        ((2, STEPS * 2 * depth, shots * CAP), bf16),
        ((2, width, shots * CAP), bf16),
    ]
    passed = [state] * 4 + [((width, width), bf16)]
    passed += ([injection] + factors) if few else [injection] * chunks
    scratch = [] if few else [pltpu.VMEM(*factor) for factor in factors]
    scratch += [
        pltpu.VMEM((slabs, shots, 2, ROWS, LANES), bf16),
        pltpu.VMEM((shots, 2, ROWS, LANES), bf16),
        pltpu.VMEM((slabs, 2, depth, width), f32),
        pltpu.VMEM(velocity.shape, bf16),
        pltpu.VMEM((3 * ROWS, NS), bf16),
        pltpu.VMEM((rows, NS), bf16),
        pltpu.VMEM((1, rows), i32),
        pltpu.VMEM((1, rows), i32),
        pltpu.VMEM((shots * LANES, width), bf16),
        dma((7,)), dma((shots,)), dma((shots,)), dma((2, slabs)), dma((2, slabs)),
        dma((slabs, shots)), dma((slabs, shots)),
    ]
    held = sum(math.prod(shape) * jnp.dtype(kind).itemsize for shape, kind in passed)
    room = (63 << 20) - (held + (1 << 20) - 1 >> 20 << 20)
    prepared = pl.pallas_call(
        exchange,
        out_shape=[pltpu.VMEM(*each) for each in passed],
        in_specs=[hbm] * 7 + [smem] * 2,
        out_specs=[vmem] * len(passed),
        scratch_shapes=scratch,
        compiler_params=pltpu.CompilerParams(
            collective_id=0, has_side_effects=True, vmem_limit_bytes=room
        ),
    )(
        split_table(), field_now, field_before, velocity, traces[0],
        trace_shot.reshape(1, rows), trace_node_cell, offsets, source_cell,
    )
    later = [pltpu.VMEM(*injection)] * (chunks - 1) if few else []
    return pl.pallas_call(
        wave,
        out_shape=jax.ShapeDtypeStruct((depth, width), f32),
        in_specs=[smem] + [vmem] * len(passed),
        out_specs=vmem,
        scratch_shapes=later + [pltpu.VMEM(*state)] * 2,
        compiler_params=pltpu.CompilerParams(vmem_limit_bytes=32 << 20),
    )(source_cell, *prepared)


def solution(mesh):
    in_specs = (
        P("slab", ("groups", "shot")),
        P("slab", ("groups", "shot")),
        P("slab", ("groups", "shot")),
        P(("groups", "shot")),
        P(("groups", "shot")),
        P("slab", ("groups", "shot"), None),
        P("slab", ("groups", "shot"), None),
        P("slab", ("groups", "shot")),
    )
    out_specs = P("slab", ("groups", "shot"))
    return jax.shard_map(local, mesh=mesh, in_specs=in_specs, out_specs=out_specs, check_vma=False)
```

```python
import math

import jax
import jax.numpy as jnp
import numpy as np
from jax import lax
from jax.experimental import pallas as pl
from jax.experimental.pallas import tpu as pltpu
from jax.sharding import PartitionSpec as P

NS = 256
STEPS = 24
CAP = 64
LANES = 128
SUB = 8
ROWS = 32
CHUNK = 4
SCRATCH = 16

LAP_CENTER = -205.0 / 72.0
LAP_TAPS = (1.6, -0.2, 8.0 / 315.0, -1.0 / 560.0)
PEAK = 0.12
DELAY = 5.0
SOURCE_GAIN = 2.0
RATIO = 0.1
NT = (((1,), (1,)), ((), ()))
MESH = pl.DeviceIdType.MESH


def dot_nt(a, b):
    return lax.dot_general(a, b, NT, preferred_element_type=jnp.float32)


def dot_nn(a, b):
    return jnp.dot(a, b, preferred_element_type=jnp.float32)


def iota(shape, axis):
    return lax.broadcasted_iota(jnp.int32, shape, axis)


def ones_where(mask):
    return jnp.where(mask, 1.0, 0.0).astype(jnp.bfloat16)


def split3(x):
    high = x.astype(jnp.bfloat16)
    rest = x - high.astype(jnp.float32)
    middle = rest.astype(jnp.bfloat16)
    low = (rest - middle.astype(jnp.float32)).astype(jnp.bfloat16)
    return jnp.concatenate([high, middle, low], axis=0)


def sum3(parts):
    n = parts.shape[0] // 3
    return parts[0:n] + parts[n : 2 * n] + parts[2 * n : 3 * n]


def split_table():
    k = np.arange(NS, dtype=np.float64)[:, None] + 0.5
    t = np.arange(STEPS, dtype=np.float64)[None, :] + 1.0
    table = np.cos(math.pi * k * t / NS) * math.sqrt(2.0 / NS)
    rest = np.zeros((ROWS, NS), np.float32)
    rest[:STEPS] = table.T
    parts = []
    for _ in range(3):
        part = rest.astype(jnp.bfloat16)
        parts.append(part)
        rest = rest - part.astype(np.float32)
    return jnp.asarray(np.concatenate(parts, axis=0))


def ricker_value(step):
    a = (math.pi * PEAK * (step - DELAY)) ** 2
    return SOURCE_GAIN * (1.0 - 2.0 * a) * math.exp(-a)


def loop(start, stop, body, unrolled):
    if unrolled:
        for i in range(start, stop):
            body(i)
        return

    def one(i, carry):
        body(i)
        return carry

    lax.fori_loop(start, stop, one, 0)


def places(j, slabs, depth):
    groups = depth * slabs // SUB
    out = []
    for q in range(depth // SUB):
        at = j * depth + q * SUB
        out.append(pl.ds((at % groups) * SUB + at // groups, SUB, stride=SUB))
    return out


def source_at(source, columns):
    width = columns * LANES
    return source // width, source % width % columns, source % width // columns


def put_product(chunk, e, slabs, left, right, injection, extra):
    half, chunk_rows = e % 2, left.shape[1] // (STEPS // CHUNK)
    depth, columns = chunk_rows // (2 * CHUNK), right.shape[1] // LANES
    j = lax.rem(lax.axis_index("slab") + e, slabs)
    begin = chunk * chunk_rows
    product = dot_nt(left[half, begin : begin + chunk_rows, :], right[half])
    for q, place in enumerate(places(j, slabs, depth)):
        for t in range(CHUNK):
            at = 2 * t * depth + q * SUB
            block = product[at : at + SUB] + product[at + depth : at + depth + SUB]
            if extra is not None:
                block = block + ricker_value(float(chunk * CHUNK + t)) * extra[q]
            for c in range(columns):
                injection[t, c, place, :] = block[:, c * LANES : (c + 1) * LANES]


def exchange_kernel(
    shots, slabs, table_hbm, now_hbm, before_hbm, velocity_hbm, traces_hbm, shot_hbm, node_hbm,
    offset_ref, source_ref, *refs,
):
    few = slabs <= 2 and shots <= 8
    chunks = STEPS // CHUNK
    count = SCRATCH if few else SCRATCH + 2
    outs, scratch = refs[:-count], refs[-count:]
    first, second, scale, center, perm = outs[:5]
    injections = outs[5:6] if few else outs[5 : 5 + chunks]
    (
        left, right, gathered, message, raw, panel_ref, table_ref, traces_ref, shot_ref, node_ref,
        window, load_sem, send_sem, recv_sem, field_send, field_recv, relay_send, relay_recv,
    ) = (outs[6:8] + scratch) if few else scratch
    shot, slab = lax.axis_index("shot"), lax.axis_index("slab")
    depth, width = now_hbm.shape
    rows = traces_ref.shape[0]
    columns = width // LANES
    groups = depth * slabs // SUB

    def other_shot(d):
        return {"shot": lax.rem(shot + d, shots)}

    def other_slab(e):
        return {"slab": lax.rem(slab + e, slabs)}

    def load(i, source, to):
        return pltpu.make_async_copy(source, to, load_sem.at[i])

    load_traces = [
        load(0, traces_hbm, traces_ref), load(1, shot_hbm, shot_ref),
        load(2, node_hbm, node_ref), load(3, table_hbm, table_ref),
    ]
    load_panel = load(4, velocity_hbm, panel_ref)
    load_fields = [load(5, now_hbm, raw.at[slab, 0]), load(6, before_hbm, raw.at[slab, 1])]
    for copy in load_traces + [load_panel] + load_fields:
        copy.start()

    barrier = pltpu.get_barrier_semaphore()

    def greet_shot(d):
        pl.semaphore_signal(barrier, inc=1, device_id=other_shot(d), device_id_type=MESH)

    def greet_slab(e):
        pl.semaphore_signal(barrier, inc=1, device_id=other_slab(e), device_id_type=MESH)

    loop(1, slabs, greet_slab, few)
    loop(1, shots, greet_shot, few)

    def remote(source, to, send, recv, device):
        return pltpu.make_async_remote_copy(
            src_ref=source, dst_ref=to, send_sem=send, recv_sem=recv,
            device_id=device, device_id_type=MESH,
        )

    def field_copy(e, i):
        return remote(
            now_hbm if i == 0 else before_hbm, raw.at[slab, i],
            field_send.at[i, e], field_recv.at[i, e], other_slab(e),
        )

    def message_copy(d):
        return remote(
            message.at[lax.rem(shot + d, shots)], gathered.at[slab, shot],
            send_sem.at[d], recv_sem.at[d], other_shot(d),
        )

    def relay_copy(d, e):
        source = lax.rem(shot + shots - d, shots)
        return remote(
            gathered.at[slab, source], gathered.at[slab, source],
            relay_send.at[e, d], relay_recv.at[e, d], other_slab(e),
        )

    lane = iota((1, width), 1)
    spread_lane = (lane % LANES) * columns + lane // LANES
    perm[...] = ones_where(iota((width, width), 0) == spread_lane)
    ahead = ones_where(iota((rows, rows), 0) < iota((rows, rows), 1))
    offset = offset_ref[0]
    first_cell = spread_lane + offset

    def open_window(s):
        begin = s * LANES
        if not isinstance(s, int):
            begin = pl.multiple_of(begin, LANES)
        window[pl.ds(begin, LANES), :] = ones_where(
            iota((LANES, width), 0) + begin == first_cell
        )

    loop(0, shots, open_window, few)

    for copy in load_traces + [load_panel]:
        copy.wait()
    amplitude = sum3(dot_nt(table_ref[...], traces_ref[...]))
    node = node_ref[...]
    lateral = node % width
    row = iota((ROWS, rows), 0)
    where_to = jnp.where(
        row == STEPS, node // width,
        jnp.where(row == STEPS + 1, lateral // columns, lateral % columns),
    ).astype(jnp.float32)
    high = jnp.where(row < STEPS, amplitude, where_to).astype(jnp.bfloat16)
    low = jnp.where(row < STEPS, amplitude - high.astype(jnp.float32), where_to).astype(
        jnp.bfloat16
    )
    both = jnp.concatenate([high, low], axis=0)
    target = shot_ref[...]
    onehot = jnp.where(iota((shots, rows), 0) == target, 1.0, 0.0)
    count = dot_nn(onehot.astype(jnp.bfloat16), ahead)
    position = jnp.sum(onehot * count, axis=0, keepdims=True)
    slot = position + (target * CAP).astype(jnp.float32)
    at_slot = iota((LANES, rows), 0).astype(jnp.float32)
    low_half = iota((ROWS, LANES), 1) < CAP

    def fill(i):
        base = (i * LANES).astype(jnp.float32) if not isinstance(i, int) else float(i * LANES)
        picked = dot_nt(both, ones_where(at_slot == slot - base))
        highs, lows = picked[0:ROWS], picked[ROWS : 2 * ROWS]
        message[2 * i, 1] = panel_ref[...]
        message[2 * i + 1, 1] = panel_ref[...]
        message[2 * i, 0] = jnp.where(low_half, highs, pltpu.roll(lows, CAP, 1)).astype(jnp.bfloat16)
        message[2 * i + 1, 0] = jnp.where(low_half, pltpu.roll(highs, CAP, 1), lows).astype(
            jnp.bfloat16
        )

    loop(0, shots // 2, fill, few)
    pl.semaphore_wait(barrier, shots - 1 + slabs - 1)
    loop(1, shots, lambda d: message_copy(d).start(), few)

    def start_fields(e):
        field_copy(e, 0).start()
        field_copy(e, 1).start()

    loop(1, slabs, start_fields, few)
    gathered[slab, shot] = message[shot]
    loop(1, slabs, lambda e: relay_copy(0, e).start(), few)

    def put(ref, j, values):
        for q, place in enumerate(places(j, slabs, depth)):
            for c in range(columns):
                ref[c, place, :] = values[
                    q * SUB : (q + 1) * SUB, c * LANES : (c + 1) * LANES
                ]

    def put_fields(j):
        both_fields = jnp.concatenate([raw[j, 0], raw[j, 1]], axis=0)
        turned = sum3(dot_nn(split3(both_fields), perm[...]))
        put(first, j, turned[0:depth])
        put(second, j, turned[depth : 2 * depth])

    for copy in load_fields:
        copy.wait()
    put_fields(slab)

    row_depth = iota((depth, LANES), 0).astype(jnp.float32)
    at_lane = iota((LANES, LANES), 0).astype(jnp.float32)

    low_lanes = iota((ROWS, LANES), 1) < CAP

    def build(e, i):
        half = e % 2
        j = lax.rem(slab + e, slabs)
        lanes = pl.ds(i * LANES if isinstance(i, int) else pl.multiple_of(i * LANES, LANES), LANES)
        one = gathered[j, 2 * i, 0].astype(jnp.float32)
        two = gathered[j, 2 * i + 1, 0].astype(jnp.float32)
        parts = (
            jnp.where(low_lanes, one, pltpu.roll(two, CAP, 1)),
            jnp.where(low_lanes, pltpu.roll(one, CAP, 1), two),
        )
        chosen = ones_where(row_depth == parts[0][STEPS : STEPS + 1])
        for t in range(STEPS):
            for h in range(2):
                spread = jnp.broadcast_to(parts[h][t : t + 1], (2 * SUB, LANES))
                spread = spread.astype(jnp.bfloat16)
                for part in range(0, depth, 2 * SUB):
                    at = (2 * t + h) * depth + part
                    left[half, at : at + 2 * SUB, lanes] = (
                        chosen[part : part + 2 * SUB] * spread
                    )
        lane_at, column_at = parts[0][STEPS + 1 : STEPS + 2], parts[0][STEPS + 2 : STEPS + 3]
        for c in range(columns):
            key = jnp.where(column_at == float(c), lane_at, -1.0)
            right[half, c * LANES : (c + 1) * LANES, lanes] = ones_where(at_lane == key)

    source_depth, source_column, source_lane = source_at(source_ref[0], columns)
    here = iota((SUB, width), 1) == source_column * LANES + source_lane

    def put_injection(e, chunk):
        j = lax.rem(slab + e, slabs)
        extra = [
            jnp.where((iota((SUB, width), 0) + (q * SUB + j * depth) == source_depth) & here, 1.0, 0.0)
            for q in range(depth // SUB)
        ]
        put_product(chunk, e, slabs, left, right, injections[chunk], extra)

    def wait_fields(e):
        field_copy(e, 0).wait()
        field_copy(e, 1).wait()
        put_fields(lax.rem(slab + slabs - e, slabs))

    loop(1, slabs, wait_fields, few)

    def arrive(s):
        d = lax.rem(shot + shots - s, shots)

        @pl.when(d > 0)
        def _():
            message_copy(d).wait_recv()
            loop(1, slabs, lambda e: relay_copy(d, e).start(), few)

    def arrive_pair(i):
        arrive(2 * i)
        arrive(2 * i + 1)
        build(0, i)

    loop(0, shots // 2, arrive_pair, few)

    def put_courant(j):
        panel = jnp.concatenate(
            [gathered[j, s, 1] for s in range(shots)], axis=1
        )
        speed = dot_nn(panel, window[...]) * RATIO
        courant = speed * speed
        put(scale, j, courant * LAP_TAPS[0])
        put(center, j, courant * (2.0 * LAP_CENTER) + 2.0)

    if not few:
        put_courant(slab)
    if not few:
        put_injection(0, 0)

    def put_courants():
        panel = jnp.concatenate(
            [
                jnp.concatenate([gathered[j, s, 1] for s in range(shots)], axis=1)
                for j in range(slabs)
            ],
            axis=0,
        )
        speed = dot_nn(panel, window[...]) * RATIO
        courant = speed * speed
        for j in range(slabs):
            mine = courant[j * depth : (j + 1) * depth]
            put(scale, j, mine * LAP_TAPS[0])
            put(center, j, mine * (2.0 * LAP_CENTER) + 2.0)

    def relay_arrive(e, s):
        relay_copy(lax.rem(shot + shots - s, shots), e).wait_recv()

    def relay_pair(e, i):
        relay_arrive(e, 2 * i)
        relay_arrive(e, 2 * i + 1)
        build(e, i)

    if few:
        for e in range(1, slabs):
            loop(0, shots // 2, lambda i: relay_pair(e, i), True)
        put_courants()
        for e in range(slabs):
            put_injection(e, 0)
    else:
        for chunk in range(1, chunks):
            put_injection(0, chunk)

        def finish(e):
            loop(0, shots, lambda d: relay_copy(d, e).wait_recv(), False)

        def others(e):
            loop(0, shots // 2, lambda i: build(e, i), False)
            put_courant(lax.rem(slab + e, slabs))
            for chunk in range(chunks):
                put_injection(e, chunk)

        loop(1, slabs, finish, False)
        loop(1, slabs, others, False)
    loop(1, shots, lambda d: message_copy(d).wait_send(), few)
    loop(0, shots, lambda d: loop(1, slabs, lambda e: relay_copy(d, e).wait_send(), few), few)


def advance(injection, scale, center, t, now, earlier, later):
    columns, groups = now.shape[0], now.shape[1] // SUB
    lane, sub = iota((SUB, LANES), 1), iota((SUB, LANES), 0)

    def cell(c, v):
        return now[c, v * SUB : (v + 1) * SUB, :]

    line = {(c, v): cell(c, v) for c in range(columns) for v in range(groups)}
    for c in range(columns):
        for k in range(4):
            line[c, groups + k] = jnp.where(
                sub < SUB - 1, pltpu.roll(cell(c, k), SUB - 1, 0), 0.0
            )
            line[c, k - 4] = jnp.where(
                sub > 0, pltpu.roll(cell(c, groups + k - 4), 1, 0), 0.0
            )
    for v in range(groups):
        mine = [line[c, v] for c in range(columns)]
        plus = [jnp.where(lane < LANES - 1, pltpu.roll(x, LANES - 1, 1), 0.0) for x in mine]
        minus = [jnp.where(lane > 0, pltpu.roll(x, 1, 1), 0.0) for x in mine]
        rows = slice(v * SUB, (v + 1) * SUB)
        for c in range(columns):
            total = None
            for k in range(1, 5):
                after = mine[c + k] if c + k < columns else plus[c + k - columns]
                prior = mine[c - k] if c >= k else minus[c - k + columns]
                taps = (after + prior) + (line[c, v + k] + line[c, v - k])
                if k == 1:
                    total = taps
                else:
                    total = total + (LAP_TAPS[k - 1] / LAP_TAPS[0]) * taps
            later[c, rows, :] = (
                (center[c, rows, :] * mine[c] - earlier[c, rows, :])
                + scale[c, rows, :] * total
                + injection[t, c, rows, :]
            )


def wave_kernel(shots, slabs, source_ref, first, second, scale, center, perm, *refs):
    few = slabs <= 2 and shots <= 8
    chunks = STEPS // CHUNK
    if few:
        opening, left, right, out_ref = refs[:4]
        injections = (opening,) + refs[4 : 3 + chunks]
    else:
        injections, out_ref = refs[:chunks], refs[chunks]
    states = refs[-2:]
    depth, width = out_ref.shape
    columns = width // LANES
    groups = depth * slabs // SUB
    slab = lax.axis_index("slab")
    source_depth, source_column, source_lane = source_at(source_ref[0], columns)
    source_row = (source_depth % groups) * SUB + source_depth // groups
    here = iota((1, LANES), 1) == source_lane

    def prepare(chunk):
        injection = injections[chunk]
        for e in range(slabs):
            put_product(chunk, e, slabs, left, right, injection, None)
        for t in range(CHUNK):
            spot = pl.ds(source_row, 1)
            value = ricker_value(float(chunk * CHUNK + t))
            injection[t, source_column, spot, :] = injection[t, source_column, spot, :] + jnp.where(
                here, value, 0.0
            )

    for chunk in range(chunks):
        if few and chunk + 1 < chunks:
            prepare(chunk + 1)

        def step(t, now, before, after):
            advance(injections[chunk], scale, center, t, now, before, after)

        if chunk == 0:
            step(0, first, second, states[0])
            step(1, states[0], first, states[1])

        def pair(i):
            step(2 * i, states[1], states[0], states[0])
            step(2 * i + 1, states[0], states[1], states[1])

        loop(1 if chunk == 0 else 0, CHUNK // 2, pair, few)

    mine = jnp.concatenate(
        [
            jnp.concatenate([states[1][c, place, :] for c in range(columns)], axis=1)
            for place in places(slab, slabs, depth)
        ],
        axis=0,
    )
    out_ref[...] = sum3(dot_nt(split3(mine), perm[...]))


def local(
    field_now, field_before, velocity, offsets, source_cell, traces, trace_shot, trace_node_cell
):
    depth, width = field_now.shape
    shots, slabs = lax.axis_size("shot"), lax.axis_size("slab")
    rows = traces.shape[1]
    columns = width // LANES
    cells = depth * slabs
    vmem = pl.BlockSpec(memory_space=pltpu.VMEM)
    hbm = pl.BlockSpec(memory_space=pltpu.HBM)
    dma = pltpu.SemaphoreType.DMA
    f32, bf16, i32 = jnp.float32, jnp.bfloat16, jnp.int32

    chunks = STEPS // CHUNK
    few = slabs <= 2 and shots <= 8
    smem = pl.BlockSpec(memory_space=pltpu.SMEM)

    def exchange(*refs):
        exchange_kernel(shots, slabs, *refs)

    def wave(*refs):
        wave_kernel(shots, slabs, *refs)

    state = ((columns, cells, LANES), f32)
    injection = ((CHUNK, columns, cells, LANES), f32)
    factors = [
        ((2, STEPS * 2 * depth, shots * CAP), bf16),
        ((2, width, shots * CAP), bf16),
    ]
    passed = [state] * 4 + [((width, width), bf16)]
    passed += ([injection] + factors) if few else [injection] * chunks
    scratch = [] if few else [pltpu.VMEM(*factor) for factor in factors]
    scratch += [
        pltpu.VMEM((slabs, shots, 2, ROWS, LANES), bf16),
        pltpu.VMEM((shots, 2, ROWS, LANES), bf16),
        pltpu.VMEM((slabs, 2, depth, width), f32),
        pltpu.VMEM(velocity.shape, bf16),
        pltpu.VMEM((3 * ROWS, NS), bf16),
        pltpu.VMEM((rows, NS), bf16),
        pltpu.VMEM((1, rows), i32),
        pltpu.VMEM((1, rows), i32),
        pltpu.VMEM((shots * LANES, width), bf16),
        dma((7,)), dma((shots,)), dma((shots,)), dma((2, slabs)), dma((2, slabs)),
        dma((slabs, shots)), dma((slabs, shots)),
    ]
    held = sum(math.prod(shape) * jnp.dtype(kind).itemsize for shape, kind in passed)
    room = (63 << 20) - (held + (1 << 20) - 1 >> 20 << 20)
    prepared = pl.pallas_call(
        exchange,
        out_shape=[pltpu.VMEM(*each) for each in passed],
        in_specs=[hbm] * 7 + [smem] * 2,
        out_specs=[vmem] * len(passed),
        scratch_shapes=scratch,
        compiler_params=pltpu.CompilerParams(
            collective_id=0, has_side_effects=True, vmem_limit_bytes=room
        ),
    )(
        split_table(), field_now, field_before, velocity, traces[0],
        trace_shot.reshape(1, rows), trace_node_cell, offsets, source_cell,
    )
    later = [pltpu.VMEM(*injection)] * (chunks - 1) if few else []
    return pl.pallas_call(
        wave,
        out_shape=jax.ShapeDtypeStruct((depth, width), f32),
        in_specs=[smem] + [vmem] * len(passed),
        out_specs=vmem,
        scratch_shapes=later + [pltpu.VMEM(*state)] * 2,
        compiler_params=pltpu.CompilerParams(vmem_limit_bytes=32 << 20),
    )(source_cell, *prepared)


def solution(mesh):
    in_specs = (
        P("slab", ("groups", "shot")),
        P("slab", ("groups", "shot")),
        P("slab", ("groups", "shot")),
        P(("groups", "shot")),
        P(("groups", "shot")),
        P("slab", ("groups", "shot"), None),
        P("slab", ("groups", "shot"), None),
        P("slab", ("groups", "shot")),
    )
    out_specs = P("slab", ("groups", "shot"))
    return jax.shard_map(local, mesh=mesh, in_specs=in_specs, out_specs=out_specs, check_vma=False)
```
